128 devices in a mesh: tok: 16 (over x, z), head: 8 (over y, core).
Axes of the slice: x: 4, y: 4, z: 4, core: 2. Of those that a mesh axis runs over, the one named last changes fastest.
Arguments:
- tokens: bfloat16 [4096, 2880], P(('tok', 'head')), may hold values from -6 to 6
- lengths: int32 [4], replicated, may hold values from 1 to 2048, 3968 in all
- norm_gain_attn: float32 [2880], replicated, may hold values from 0.1 to 1.9
- query_key_value_weight: bfloat16 [2880, 5120], P(None, 'head'), may hold values from -0.109375 to 0.109375
- sinks: float32 [64], P('head'), may hold values from 1 to 6
- w_out_attn: bfloat16 [4096, 2880], P('head'), may hold values from -0.09375 to 0.09375
- norm_gain_moe: float32 [2880], replicated, may hold values from 0.1 to 1.9
- routes: int32 [4096, 4], P(('tok', 'head')), may hold values from 0 to 31, all different within a row; in each aligned block of 32 rows (0 to 31, 32 to 63, ...) at most 6 rows name the same one
- gates: float32 [4096, 4], P(('tok', 'head')), may hold values from 0.1 to 1
- w_in: bfloat16 [128, 2880, 1440], P(('tok', 'head')), may hold values from -0.109375 to 0.109375
- w_down: bfloat16 [128, 720, 2880], P(('tok', 'head')), may hold values from -0.109375 to 0.109375
- page_table: int32 [256], replicated, may hold values from 0 to 255, as said below
Outputs:
- hidden_out: bfloat16 [4096, 2880], P(('tok', 'head'))
- kv_cache: bfloat16 [8, 256, 16, 128], P('head', 'tok')
The draws below stay inside these ranges and needn't reach their ends.
Inputs may be any that keep to these rules, and one draw needn't show every extreme that they name: `routes`: every row names 4 different experts. In each aligned block of 32 rows no expert is named by more than 6 rows, and in every draw some block has an expert named by exactly 6 rows. `lengths`: they sum to 3968, and the longest is exactly 2048. `page_table`: A permutation. Of the 16 logical pages in each aligned block of 16, exactly 1 map into each aligned block of 16 physical pages.
All inputs are finite; a program needn't handle non-finite values.
Results may differ from the reference program's by a relative error of at most 0.018.
Values may be sent and summed in bfloat16 or wider, within the bound.
A program may use at most 128 MiB of HBM per device.

```python
import math
import jax
import jax.numpy as jnp
import numpy as np
from jax import lax

MODEL_WIDTH = 2880
NQ = 64
KEY_VALUE_HEADS = 8
HEAD_SIZE = 64
EXPERTS = 32
TOPK = 4
FF = 2880
ATTEND_WINDOW = 128
NSEQ = 4
PAGE_TOKENS = 16
QUERY_PER_KEY = 8
SPLIT = 4
FFS = 720
PACKED_TOKENS = 4096
ROWS = 32
VALID = 3968
LONGEST = 2048
CAP = 6
CACHE_PAGES = 256
PAGES_DEV = 16
PAGE_SHARE = 1


def shuffle(subkey):
    return jax.random.permutation(subkey, PAGES_DEV)


def draw_page_table(key, part):
    blocks = CACHE_PAGES // PAGES_DEV
    source_keys = jax.random.split(jax.random.fold_in(key, 11), blocks)
    target_keys = jax.random.split(jax.random.fold_in(key, 12), blocks)
    spread = jax.vmap(shuffle)(source_keys).astype(jnp.int32)
    landing = jax.vmap(shuffle)(target_keys).astype(jnp.int32)
    target = spread // PAGE_SHARE
    within = spread % PAGE_SHARE
    anchor = jnp.arange(blocks, dtype=jnp.int32)[:, None]
    placed_slot = landing[target, anchor * PAGE_SHARE + within]
    return (target * PAGES_DEV + placed_slot).reshape(-1).astype(jnp.int32)


def block_scale(key, dims, shards, least, high):
    gain, own = 1.0, jax.random.fold_in(key, 6)
    for dim, blocks in shards:
        heights = jnp.exp(jax.random.uniform(jax.random.fold_in(own, dim), (blocks,), jnp.float32, least / len(shards), high / len(shards)))
        gain = gain * jnp.repeat(heights, dims[dim] // blocks).reshape([-1 if axis == dim else 1 for axis in range(len(dims))])
    return gain


def length_profile(count, total, bound, lean):
    weights = [(1 << 20) // math.isqrt(grade ** lean) + 1 for grade in range(2, count + 1)]
    rest, holding = total - bound - (count - 1), [1] * (count - 1)
    while rest > 0:
        movable = [i for i in range(count - 1) if holding[i] < bound]
        mass, left = sum([weights[i] for i in movable]), rest
        for i in movable:
            addition = min(bound - holding[i], max(1, left * weights[i] // mass), rest)
            holding[i] = holding[i] + addition
            rest = rest - addition
    return np.array([bound] + holding)


def ragged_sizes(rng, amount, total, limit, slope):
    if amount == 2:
        one = jax.random.randint(rng, (), max(1, total - limit), min(limit, total - 1) + 1)
        return jnp.stack([one, total - one])
    tallies = jnp.asarray(length_profile(amount, total, limit, slope), jnp.int32)
    couples = (amount - 1) // 2
    giver, taker = tallies[1:1 + 2 * couples:2], tallies[2:2 + 2 * couples:2]
    slack = jnp.minimum(giver - 1, limit - taker)
    moved = jax.random.randint(jax.random.fold_in(rng, 1), (couples,), 0, 1 << 20) % (slack + 1)
    tallies = tallies.at[1:1 + 2 * couples:2].set(giver - moved).at[2:2 + 2 * couples:2].set(taker + moved)
    return tallies[jax.random.permutation(jax.random.fold_in(rng, 2), amount)]


def deal_out(key, own, number, rows, number_of, top, limit, skew):
    order = jax.random.permutation(key, number_of)
    crowded, common = load_shares(number_of, rows * top, limit, skew, True), load_shares(number_of, rows * top, limit, skew, False)
    places = jnp.arange(number_of)

    def named(sizes, offset_by):
        used = int((sizes > 0).sum())
        fixed = max(1, used // 4)
        moved = fixed + (places - fixed + offset_by * (used - fixed)) % max(1, number_of - fixed)
        return jnp.zeros((number_of,), jnp.int32).at[order[jnp.where(places < fixed, places, moved)]].set(jnp.asarray(sizes, jnp.int32))

    sizes = jnp.where(number % 4 == 0, named(crowded, number // 4), named(common, number - number // 4 - 1))
    mixed = jax.random.permutation(jax.random.fold_in(own, 3), number_of)
    giver, receiver = mixed[0:number_of // 2 * 2:2], mixed[1:number_of // 2 * 2:2]
    slack = jnp.minimum(sizes[giver] - 1, limit - sizes[receiver]) // 2
    slack = jnp.where((giver == order[0]) | (receiver == order[0]) | (sizes[receiver] == 0), 0, jnp.maximum(slack, 0))
    moved = jax.random.randint(jax.random.fold_in(own, 4), (number_of // 2,), 0, 1 << 20) % (slack + 1)
    sizes = sizes.at[giver].add(-moved).at[receiver].add(moved)
    items = jnp.searchsorted(jnp.cumsum(sizes), jnp.arange(rows * top), side="right").astype(jnp.int32)
    grid = items.reshape(top, rows).T
    grid = grid[jax.random.permutation(jax.random.fold_in(own, 1), rows)]
    offset_by = jax.random.randint(jax.random.fold_in(own, 2), (rows, 1), 0, top)
    return jnp.take_along_axis(grid, (jnp.arange(top)[None, :] + offset_by) % top, axis=1)


def load_shares(count, total, limit, lean, full):
    portions = [(1 << 20) // math.isqrt(standing ** lean) + 1 for standing in range(1, count + 1)]
    largest = limit if full else min(limit, max(-(-total // count), total * portions[0] // sum(portions)))
    least = 1 if total - largest >= count - 1 else 0
    holding, surplus = [largest] + [least] * (count - 1), total - largest - least * (count - 1)
    while surplus > 0:
        movable = [i for i in range(1, count) if holding[i] < largest] or [i for i in range(1, count) if holding[i] < limit]
        mass, left = sum([portions[i] for i in movable]), surplus
        for i in movable:
            addition = min(limit - holding[i], max(1, left * portions[i] // mass), surplus)
            holding[i] = holding[i] + addition
            surplus = surplus - addition
    return np.array(holding)


def normal_values(own_key, extent, width, reach, cuts=(), kind=jnp.bfloat16):
    array = jax.random.normal(own_key, extent, jnp.float32) * width
    if len(cuts) > 0:
        array = block_scale(own_key, extent, cuts, -0.22, 0.18) * array
    return jnp.clip(array, min=-reach, max=reach).astype(kind)


def setup_inputs(seed: int = 0) -> dict:
    seeds = jax.random.split(jax.random.key(seed), 13)
    tokens = normal_values(seeds[0], (PACKED_TOKENS, MODEL_WIDTH), 1.0, 6.0, ((0, 128),))
    lengths = ragged_sizes(seeds[1], NSEQ, VALID, LONGEST, 2).astype(jnp.int32)
    norm_gain_attn = jnp.clip(1.0 + 0.18 * jax.random.normal(seeds[2], (MODEL_WIDTH,), jnp.float32), 0.1, 1.9)
    query_key_value_weight = normal_values(seeds[3], (MODEL_WIDTH, KEY_VALUE_HEADS * (QUERY_PER_KEY + 2) * HEAD_SIZE), MODEL_WIDTH ** -0.5, 0.109375, ((1, 8),))
    sinks = jnp.clip(1.0 + 5.0 * jax.random.uniform(seeds[4], (NQ,), jnp.float32) ** block_scale(seeds[4], (NQ,), ((0, 8),), -0.2, 0.2), 1.0, 6.0)
    w_out_attn = normal_values(seeds[5], (NQ * HEAD_SIZE, MODEL_WIDTH), (NQ * HEAD_SIZE) ** -0.5, 0.09375, ((0, 8),))
    norm_gain_moe = jnp.clip(1.0 + 0.18 * jax.random.normal(seeds[6], (MODEL_WIDTH,), jnp.float32), 0.1, 1.9)
    routes_keys = jax.random.split(jax.random.fold_in(seeds[7], 1), PACKED_TOKENS // ROWS)
    routes_turns = jax.random.permutation(jax.random.fold_in(seeds[7], 3), PACKED_TOKENS // ROWS)
    routes = jax.vmap(lambda own, number: deal_out(jax.random.fold_in(seeds[7], 2), own, number, ROWS, EXPERTS, TOPK, CAP, 1))(routes_keys, routes_turns).reshape((PACKED_TOKENS, TOPK))
    gates = jnp.clip(0.1 + 0.9 * jax.random.uniform(seeds[8], (PACKED_TOKENS, TOPK), jnp.float32) ** block_scale(seeds[8], (PACKED_TOKENS, TOPK), ((0, 128),), -0.2, 0.2), 0.1, 1.0)
    w_in = normal_values(seeds[9], (EXPERTS * SPLIT, MODEL_WIDTH, 2 * FFS), MODEL_WIDTH ** -0.5, 0.109375, ((0, 128),))
    w_down = normal_values(seeds[10], (EXPERTS * SPLIT, FFS, MODEL_WIDTH), FF ** -0.5, 0.109375, ((0, 128),))
    page_table = draw_page_table(jax.random.fold_in(seeds[12], 71), 0)
    return dict(tokens=tokens, lengths=lengths, norm_gain_attn=norm_gain_attn, query_key_value_weight=query_key_value_weight, sinks=sinks, w_out_attn=w_out_attn, norm_gain_moe=norm_gain_moe, routes=routes, gates=gates, w_in=w_in, w_down=w_down, page_table=page_table)


EPSILON = 1e-05
ROPE_BASE = 150000.0
GLU_ALPHA = 1.702

def to_wide(values):
    return lax.optimization_barrier(values).astype(jnp.float32)

def normalize(values, gain_vec):
    wide = values.astype(jnp.float32)
    inv_rms = lax.rsqrt(lax.optimization_barrier(jnp.mean(wide * wide, axis=-1, keepdims=True)) + EPSILON)
    return wide * inv_rms * gain_vec

def segment_table(lengths, row_index):
    seq_ends = jnp.cumsum(lengths).astype(jnp.int32)
    starts = jnp.concatenate([jnp.zeros((1,), jnp.int32), seq_ends])
    segment = lax.optimization_barrier(jnp.sum((row_index[:, None] >= seq_ends[None, :]).astype(jnp.int32), axis=1)).astype(jnp.int32)
    onehot = segment[:, None] == jnp.arange(starts.shape[0], dtype=jnp.int32)[None, :]
    seg_start = lax.optimization_barrier(jnp.sum(jnp.where(onehot, starts[None, :], 0), axis=1)).astype(jnp.int32)
    return (segment, (row_index - seg_start).astype(jnp.int32))

def rotate(values, positions):
    half_dim = values.shape[-1] // 2
    inv_freq = jnp.exp(jnp.arange(half_dim, dtype=jnp.float32) * (-2.0 * math.log(ROPE_BASE) / values.shape[-1]))
    angles = positions.astype(jnp.float32)[:, None] * inv_freq[None, :]
    view_shape = (angles.shape[0],) + (1,) * (values.ndim - 2) + (half_dim,)
    cos_table = jnp.cos(angles).reshape(view_shape)
    sin_table = jnp.sin(angles).reshape(view_shape)
    lower_half = values[..., :half_dim]
    upper_half = values[..., half_dim:]
    return jnp.concatenate([lower_half * cos_table - upper_half * sin_table, upper_half * cos_table + lower_half * sin_table], axis=-1)

def band_mask(query_index, key_index, query_segs, key_segs, window):
    nblocks = query_index.shape[0] // window
    query_pos = query_index.reshape(nblocks, window)
    query_seg = query_segs.reshape(nblocks, window)
    key_grid = key_index.reshape(nblocks + 1, window)
    seg_grid = key_segs.reshape(nblocks + 1, window)
    key_pos = jnp.concatenate([key_grid[:-1], key_grid[1:]], axis=1)
    key_seg = jnp.concatenate([seg_grid[:-1], seg_grid[1:]], axis=1)
    distance = query_pos[:, :, None] - key_pos[:, None, :]
    allowed = (query_seg[:, :, None] == key_seg[:, None, :]) & (query_seg < NSEQ)[:, :, None]
    allowed = allowed & (key_pos >= 0)[:, None, :] & (distance >= 0) & (distance < window)
    return allowed

def reference(tokens, lengths, norm_gain_attn, query_key_value_weight, sinks, w_out_attn, norm_gain_moe, routes, gates, w_in, w_down, page_table):
    row_index = jnp.arange(PACKED_TOKENS, dtype=jnp.int32)
    segment, positions = segment_table(lengths, row_index)
    normed_input = normalize(tokens, norm_gain_attn).astype(jnp.bfloat16)
    projected_rows = jnp.dot(normed_input, query_key_value_weight, preferred_element_type=jnp.float32).reshape(PACKED_TOKENS, KEY_VALUE_HEADS, QUERY_PER_KEY + 2, HEAD_SIZE)
    query_rows = (rotate(projected_rows[:, :, :QUERY_PER_KEY], positions) * HEAD_SIZE ** (-0.5)).astype(jnp.bfloat16)
    key_rot = rotate(projected_rows[:, :, QUERY_PER_KEY], positions)
    key_value_pairs = jnp.concatenate([key_rot, projected_rows[:, :, QUERY_PER_KEY + 1]], axis=-1).astype(jnp.bfloat16)
    padded_rows = jnp.concatenate([jnp.zeros((ATTEND_WINDOW, KEY_VALUE_HEADS, 2 * HEAD_SIZE), jnp.bfloat16), key_value_pairs], axis=0)
    key_index = jnp.arange(PACKED_TOKENS + ATTEND_WINDOW, dtype=jnp.int32) - ATTEND_WINDOW
    key_segs, _ = segment_table(lengths, key_index)
    nblocks = PACKED_TOKENS // ATTEND_WINDOW
    allowed = band_mask(row_index, key_index, segment, key_segs, ATTEND_WINDOW)

    def single_group(operands):
        group_queries, group_pairs, group_sinks = operands
        query_blocks = to_wide(group_queries).reshape(nblocks, ATTEND_WINDOW, QUERY_PER_KEY, HEAD_SIZE)
        pair_grid = to_wide(group_pairs).reshape(nblocks + 1, ATTEND_WINDOW, 2 * HEAD_SIZE)
        key_band = jnp.concatenate([pair_grid[:-1], pair_grid[1:]], axis=1)
        scores = jnp.einsum('bqnh,bkh->bnqk', query_blocks, key_band[..., :HEAD_SIZE])
        weights = jnp.where(allowed[:, None], jnp.exp(scores), 0.0)
        totals = lax.optimization_barrier(jnp.sum(weights, axis=-1, keepdims=True)) + jnp.exp(group_sinks)[None, :, None, None]
        probs_bf = (weights / totals).astype(jnp.bfloat16)
        outputs = jnp.einsum('bnqk,bkh->bqnh', to_wide(probs_bf), key_band[..., HEAD_SIZE:])
        return outputs.astype(jnp.bfloat16).reshape(PACKED_TOKENS, QUERY_PER_KEY * HEAD_SIZE)
    group_split = lax.map(single_group, (jnp.transpose(query_rows, (1, 0, 2, 3)), jnp.transpose(padded_rows, (1, 0, 2)), sinks.reshape(KEY_VALUE_HEADS, QUERY_PER_KEY)))
    attended = jnp.transpose(group_split, (1, 0, 2)).reshape(PACKED_TOKENS, NQ * HEAD_SIZE)
    resid = tokens.astype(jnp.float32) + jnp.dot(attended, w_out_attn, preferred_element_type=jnp.float32)
    moe_in = normalize(resid, norm_gain_moe).astype(jnp.bfloat16)
    is_live = segment < NSEQ
    expert_ids = jnp.arange(EXPERTS, dtype=jnp.int32)
    naming = routes[:, :, None] == expert_ids[None, None, :]
    routed = (jnp.any(naming, axis=1) & is_live[:, None]).astype(jnp.int32)
    sources = PACKED_TOKENS // ROWS
    slot_rank = (jnp.cumsum(routed.reshape(sources, ROWS, EXPERTS), axis=1).astype(jnp.int32) - 1).reshape(PACKED_TOKENS, EXPERTS)
    slot_ids = jnp.arange(CAP, dtype=jnp.int32)
    placed = ((routed == 1)[:, :, None] & (slot_rank[:, :, None] == slot_ids[None, None, :])).reshape(sources, ROWS, EXPERTS, CAP)
    local_ids = jnp.arange(ROWS, dtype=jnp.int32)
    local_row = lax.optimization_barrier(jnp.sum(jnp.where(placed, local_ids[None, :, None, None], 0), axis=1)).astype(jnp.int32)
    global_row = (local_row + (jnp.arange(sources, dtype=jnp.int32) * ROWS)[:, None, None]).astype(jnp.int32)
    filled = jnp.any(placed, axis=1)
    weighted = jnp.where(is_live[:, None], gates, 0.0)
    expert_gate = lax.optimization_barrier(jnp.sum(jnp.where(naming, weighted[:, :, None], 0.0), axis=1))

    def one_expert(carry, operands):
        expert_in, expert_down, rows_here, filled_here, gate_here = operands
        rows_flat = rows_here.reshape(-1)
        mask_flat = filled_here.reshape(-1)
        inputs = jnp.where(mask_flat[:, None], moe_in[rows_flat], jnp.zeros((), jnp.bfloat16))
        combined = jnp.zeros((rows_flat.shape[0], MODEL_WIDTH), jnp.float32)
        for shard in range(SPLIT):
            gate_up = jnp.dot(inputs, expert_in[shard], preferred_element_type=jnp.float32)
            gate_part = gate_up[:, :FFS]
            up_part = gate_up[:, FFS:]
            activated = ((up_part + 1.0) * gate_part * jax.nn.sigmoid(GLU_ALPHA * gate_part)).astype(jnp.bfloat16)
            partial_out = jnp.dot(activated, expert_down[shard], preferred_element_type=jnp.float32).astype(jnp.bfloat16)
            combined = combined + to_wide(partial_out)
        scale_rows = jnp.where(mask_flat, gate_here[rows_flat], 0.0)
        return (carry.at[rows_flat].add(scale_rows[:, None] * combined), None)
    expert_sum, _ = lax.scan(one_expert, jnp.zeros((PACKED_TOKENS, MODEL_WIDTH), jnp.float32), (w_in.reshape(EXPERTS, SPLIT, MODEL_WIDTH, 2 * FFS), w_down.reshape(EXPERTS, SPLIT, FFS, MODEL_WIDTH), jnp.transpose(global_row, (1, 0, 2)), jnp.transpose(filled, (1, 0, 2)), jnp.transpose(expert_gate)))
    hidden_out = (resid + expert_sum).astype(jnp.bfloat16)
    page_row_slots = key_value_pairs.reshape(CACHE_PAGES, PAGE_TOKENS, KEY_VALUE_HEADS, 2 * HEAD_SIZE)
    cache = jnp.zeros_like(page_row_slots).at[page_table].set(page_row_slots)
    kv_cache = jnp.transpose(cache, (2, 0, 1, 3))
    return (hidden_out, kv_cache)
```

```python
import functools
import math

import jax
import jax.numpy as jnp
from jax import lax
from jax.experimental import pallas as pl
from jax.experimental.pallas import tpu as pltpu
from jax.sharding import PartitionSpec as P

MODEL_WIDTH = 2880
HEAD_SIZE = 64
EXPERTS = 32
ATTEND_WINDOW = 128
NSEQ = 4
PAGE_TOKENS = 16
QUERY_PER_KEY = 8


EPSILON = 1e-05
ROPE_BASE = 150000.0
GLU_ALPHA = 1.702


def passed_along(array, axis, by):
    peers = lax.axis_size(axis)
    pairs = [(i, i + by) for i in range(peers) if 0 <= i + by < peers]
    return lax.ppermute(array, axis, pairs)


def normalize(values, gain_vec):
    wide = values.astype(jnp.float32)
    inv_rms = lax.rsqrt(jnp.mean(wide * wide, axis=-1, keepdims=True) + EPSILON)
    return wide * inv_rms * gain_vec


def segment_table(lengths, row_index):
    seq_ends = jnp.cumsum(lengths)
    starts = jnp.concatenate([jnp.zeros((1,), jnp.int32), seq_ends])
    segment = jnp.sum((row_index[:, None] >= seq_ends[None, :]).astype(jnp.int32), axis=1)
    onehot = segment[:, None] == jnp.arange(starts.shape[0], dtype=jnp.int32)[None, :]
    seg_start = jnp.sum(jnp.where(onehot, starts[None, :], 0), axis=1)
    return (segment, row_index - seg_start)


def rotate(values, positions):
    half_dim = values.shape[-1] // 2
    inv_freq = jnp.exp(
        jnp.arange(half_dim, dtype=jnp.float32) * (-2.0 * math.log(ROPE_BASE) / values.shape[-1])
    )
    angles = positions.astype(jnp.float32)[:, None] * inv_freq[None, :]
    view_shape = (angles.shape[0],) + (1,) * (values.ndim - 2) + (half_dim,)
    cos_table = jnp.cos(angles).reshape(view_shape)
    sin_table = jnp.sin(angles).reshape(view_shape)
    lower_half = values[..., :half_dim]
    upper_half = values[..., half_dim:]
    return jnp.concatenate(
        [
            lower_half * cos_table - upper_half * sin_table,
            upper_half * cos_table + lower_half * sin_table,
        ],
        axis=-1,
    )


def band_mask(query_index, key_index, query_segs, key_segs, window):
    nblocks = query_index.shape[0] // window
    query_pos = query_index.reshape(nblocks, window)
    query_seg = query_segs.reshape(nblocks, window)
    key_grid = key_index.reshape(nblocks + 1, window)
    seg_grid = key_segs.reshape(nblocks + 1, window)
    key_pos = jnp.concatenate([key_grid[:-1], key_grid[1:]], axis=1)
    key_seg = jnp.concatenate([seg_grid[:-1], seg_grid[1:]], axis=1)
    distance = query_pos[:, :, None] - key_pos[:, None, :]
    allowed = (query_seg[:, :, None] == key_seg[:, None, :]) & (query_seg < NSEQ)[:, :, None]
    allowed = allowed & (key_pos >= 0)[:, None, :] & (distance >= 0) & (distance < window)
    return allowed


def band_attention(query_rows, extended, sink_table, allowed):
    nblocks = allowed.shape[0]
    groups = sink_table.shape[0]
    query_blocks = query_rows.reshape(nblocks, ATTEND_WINDOW, groups, QUERY_PER_KEY, HEAD_SIZE)
    pair_grid = extended.reshape(nblocks + 1, ATTEND_WINDOW, groups, 2 * HEAD_SIZE)
    key_band = jnp.concatenate([pair_grid[:-1], pair_grid[1:]], axis=1)
    scores = jnp.einsum(
        "bqgnh,bkgh->bgnqk",
        query_blocks,
        key_band[..., :HEAD_SIZE],
        preferred_element_type=jnp.float32,
    )
    weights = jnp.where(allowed[:, None, None], jnp.exp(scores), 0.0)
    totals = jnp.sum(weights, axis=-1, keepdims=True) + jnp.exp(sink_table)[None, :, :, None, None]
    probs_bf = (weights / totals).astype(jnp.bfloat16)
    outputs = jnp.einsum(
        "bgnqk,bkgh->bqgnh", probs_bf, key_band[..., HEAD_SIZE:], preferred_element_type=jnp.float32
    )
    return outputs.astype(jnp.bfloat16).reshape(
        nblocks * ATTEND_WINDOW, groups * QUERY_PER_KEY * HEAD_SIZE
    )


MESH = pl.DeviceIdType.MESH
VM = pltpu.VMEM
CHIPS = 64
ROWS = 32
SLOTS = 6
PARTS = 4
PART_WIDTH = MODEL_WIDTH // PARTS
CHUNK = PARTS * SLOTS
HEADS = 8


def vmem_spec():
    return pl.BlockSpec(memory_space=pltpu.VMEM)


def any_spec():
    return pl.BlockSpec(memory_space=pl.ANY)


def place():
    tok = lax.axis_index("tok")
    head = lax.axis_index("head")
    return (tok // 4, head // 2, tok % 4, head % 2)


def device(x, y, z, core):
    return (x * 4 + z, y * 2 + core)


def shifted(k, sign):
    x, y, z, core = place()
    dx, dy, dz = k // 16, (k // 4) % 4, k % 4
    if sign < 0:
        dx, dy, dz = 4 - dx, 4 - dy, 4 - dz
    return ((x + dx) % 4, (y + dy) % 4, (z + dz) % 4, core)


def sibling():
    x, y, z, core = place()
    return device(x, y, z, 1 - core)


def signal(barrier, target):
    pl.semaphore_signal(barrier, inc=1, device_id=target, device_id_type=MESH)


def greet_all(barrier):
    def greet(k, carry):
        signal(barrier, device(*shifted(k, 1)))
        return carry

    lax.fori_loop(1, CHIPS, greet, 0)
    signal(barrier, sibling())


def remote(src, dst, send, recv, target):
    return pltpu.make_async_remote_copy(
        src_ref=src, dst_ref=dst, send_sem=send, recv_sem=recv, device_id=target, device_id_type=MESH
    )


def gather_kernel(rows_ref, out_ref, send, recv, fsend, frecv, local):
    x, y, z, core = place()
    barrier = pltpu.get_barrier_semaphore()
    up = device(x, (y + 1) % 4, z, core)
    down = device(x, (y + 3) % 4, z, core)
    sib = sibling()
    for target in (up, down, sib):
        signal(barrier, target)
    pl.semaphore_wait(barrier, 3)
    mine = y * 2 + core
    lower = ((y + 3) % 4) * 2 + core
    upper = ((y + 1) % 4) * 2 + core
    far = ((y + 2) % 4) * 2 + core
    half = ROWS // 2
    first = pl.ds(0, half)
    second = pl.ds(half, half)
    to_up = remote(rows_ref, out_ref.at[mine], send.at[0], recv.at[0], up)
    to_down = remote(rows_ref, out_ref.at[mine], send.at[1], recv.at[1], down)
    to_sib = remote(rows_ref, out_ref.at[mine], fsend.at[0], frecv.at[0], sib)
    keep = pltpu.make_async_copy(rows_ref, out_ref.at[mine], local)
    to_up.start()
    to_down.start()
    to_sib.start()
    keep.start()
    to_up.wait_recv()
    on_up = remote(
        out_ref.at[lower, first], out_ref.at[lower, first], send.at[2], recv.at[2], up
    )
    on_up.start()
    sib_low = remote(out_ref.at[lower], out_ref.at[lower], fsend.at[1], frecv.at[1], sib)
    sib_low.start()
    to_down.wait_recv()
    on_down = remote(
        out_ref.at[upper, second], out_ref.at[upper, second], send.at[3], recv.at[3], down
    )
    on_down.start()
    sib_up = remote(out_ref.at[upper], out_ref.at[upper], fsend.at[2], frecv.at[2], sib)
    sib_up.start()
    on_up.wait_recv()
    on_down.wait_recv()
    sib_far = remote(out_ref.at[far], out_ref.at[far], fsend.at[3], frecv.at[3], sib)
    sib_far.start()
    for copy in (to_sib, sib_low, sib_up, sib_far):
        copy.wait()
    for copy in (to_up, to_down, on_up, on_down):
        copy.wait_send()
    keep.wait()


def gather_rows(rows):
    out = pl.pallas_call(
        gather_kernel,
        out_shape=jax.ShapeDtypeStruct((HEADS, ROWS, MODEL_WIDTH), jnp.bfloat16),
        in_specs=[vmem_spec()],
        out_specs=any_spec(),
        scratch_shapes=[
            pltpu.SemaphoreType.DMA((4,)),
            pltpu.SemaphoreType.DMA((4,)),
            pltpu.SemaphoreType.DMA((4,)),
            pltpu.SemaphoreType.DMA((4,)),
            pltpu.SemaphoreType.DMA,
        ],
        compiler_params=pltpu.CompilerParams(collective_id=0, has_side_effects=True),
        name="gather_rows",
    )(rows)
    return out.reshape(HEADS * ROWS, MODEL_WIDTH)


def reduce_kernel(part_ref, out_ref, pair_buf, sums, far_buf, psend, precv, send, recv):
    x, y, z, core = place()
    barrier = pltpu.get_barrier_semaphore()
    sib = sibling()
    signal(barrier, sib)
    for step in range(1, 4):
        signal(barrier, device(x, (y + step) % 4, z, core))
    pl.semaphore_wait(barrier, 4)
    order = (1, 2, 3, 0)
    pairs = []
    for step in order:
        owner = (y + step) % 4
        copy = remote(
            part_ref.at[owner * 2 + 1 - core], pair_buf.at[step], psend.at[step], precv.at[step], sib
        )
        copy.start()
        pairs.append(copy)
    sent = []
    for index, step in enumerate(order):
        owner = (y + step) % 4
        pairs[index].wait_recv()
        total = part_ref[owner * 2 + core].astype(jnp.float32) + pair_buf[step].astype(jnp.float32)
        if step == 0:
            own_sum = total
        else:
            sums[step] = total.astype(jnp.bfloat16)
        if index > 0:
            before = order[index - 1]
            copy = remote(
                sums.at[before],
                far_buf.at[before],
                send.at[before],
                recv.at[before],
                device(x, (y + before) % 4, z, core),
            )
            copy.start()
            sent.append(copy)
    for copy in sent:
        copy.wait_recv()
    for step in range(1, 4):
        own_sum = own_sum + far_buf[step].astype(jnp.float32)
    out_ref[...] = own_sum
    for copy in pairs + sent:
        copy.wait_send()


def sum_over_heads(part):
    return pl.pallas_call(
        reduce_kernel,
        out_shape=jax.ShapeDtypeStruct((ROWS, MODEL_WIDTH), jnp.float32),
        in_specs=[vmem_spec()],
        out_specs=vmem_spec(),
        scratch_shapes=[
            VM((4, ROWS, MODEL_WIDTH), jnp.bfloat16),
            VM((4, ROWS, MODEL_WIDTH), jnp.bfloat16),
            VM((4, ROWS, MODEL_WIDTH), jnp.bfloat16),
            pltpu.SemaphoreType.DMA((4,)),
            pltpu.SemaphoreType.DMA((4,)),
            pltpu.SemaphoreType.DMA((4,)),
            pltpu.SemaphoreType.DMA((4,)),
        ],
        compiler_params=pltpu.CompilerParams(collective_id=1, has_side_effects=True),
        name="sum_over_heads",
    )(part.reshape(HEADS, ROWS, MODEL_WIDTH))


def iota(shape, dim):
    return lax.broadcasted_iota(jnp.int32, shape, dim)


def split_index(index, size):
    whole = jnp.floor((index.astype(jnp.float32) + 0.5) * (1.0 / size)).astype(jnp.int32)
    return (whole, index - whole * size)


def prepare_kernel(sum_ref, tok_ref, gain_ref, routes_ref, live_ref, resid_ref, out_ref):
    resid = tok_ref[...].astype(jnp.float32) + sum_ref[...]
    resid_ref[...] = resid
    inv_rms = lax.rsqrt(jnp.mean(resid * resid, axis=-1, keepdims=True) + EPSILON)
    moe_in = (resid * inv_rms * gain_ref[...]).astype(jnp.bfloat16)
    expert = iota((EXPERTS, ROWS), 0)
    routed = jnp.zeros((EXPERTS, ROWS), jnp.float32)
    for k in range(4):
        routed = routed + jnp.where(routes_ref[k : k + 1, :] == expert, 1.0, 0.0)
    routed = routed * live_ref[0:1, :ROWS]
    earlier = jnp.where(iota((ROWS, ROWS), 0) < iota((ROWS, ROWS), 1), 1.0, 0.0)
    rank = jnp.dot(
        routed.astype(jnp.bfloat16), earlier.astype(jnp.bfloat16), preferred_element_type=jnp.float32
    )
    code = jnp.where(routed > 0.5, rank, -1.0).astype(jnp.bfloat16)
    count = EXPERTS * CHUNK
    owner, within = split_index(iota((count, EXPERTS), 0), CHUNK)
    spread = jnp.where(owner == iota((count, EXPERTS), 1), 1.0, 0.0).astype(jnp.bfloat16)
    code_rows = jnp.dot(spread, code, preferred_element_type=jnp.float32)
    _, within = split_index(iota((count, ROWS), 0), CHUNK)
    part, slot = split_index(within, SLOTS)
    hit = jnp.abs(code_rows - slot.astype(jnp.float32)) < 0.5
    total = jnp.zeros((count, PART_WIDTH), jnp.float32)
    for q in range(PARTS):
        pick = jnp.where(hit & (part == q), 1.0, 0.0).astype(jnp.bfloat16)
        total = total + jnp.dot(
            pick, moe_in[:, q * PART_WIDTH : (q + 1) * PART_WIDTH], preferred_element_type=jnp.float32
        )
    out_ref[...] = total.astype(jnp.bfloat16)


def prepare_chunks(attn_sum, tokens, gain, routes_t, live_row):
    resid, out = pl.pallas_call(
        prepare_kernel,
        out_shape=(
            jax.ShapeDtypeStruct((ROWS, MODEL_WIDTH), jnp.float32),
            jax.ShapeDtypeStruct((EXPERTS * CHUNK, PART_WIDTH), jnp.bfloat16),
        ),
        in_specs=[vmem_spec()] * 5,
        out_specs=(vmem_spec(), vmem_spec()),
        name="prepare_chunks",
    )(attn_sum, tokens, gain.reshape(1, MODEL_WIDTH), routes_t, live_row)
    return (resid, out.reshape(EXPERTS, CHUNK, PART_WIDTH))


def dispatch_kernel(
    out_ref, pages_ref, recv_ref, arrived_ref, send, recv, fsend, frecv, psend, precv, local
):
    x, y, z, core = place()
    tok = x * 4 + z
    barrier = pltpu.get_barrier_semaphore()
    sib = sibling()
    greet_all(barrier)
    pl.semaphore_wait(barrier, CHIPS)

    def chunk(k):
        tx, ty, tz, tc = shifted(k, 1)
        expert = (tx * 4 + tz) * 2 + ty // 2
        return remote(
            out_ref.at[expert], recv_ref.at[0, k], send.at[k], recv.at[k], device(tx, ty, tz, tc)
        )

    def page(j):
        tx, tz = (x + j // 4) % 4, (z + j % 4) % 4
        return remote(
            pages_ref.at[tx * 4 + tz],
            arrived_ref.at[tok],
            psend.at[j],
            precv.at[j],
            device(tx, y, tz, core),
        )

    def start_chunk(k, carry):
        chunk(k).start()
        return carry

    def start_page(j, carry):
        page(j).start()
        return carry

    lax.fori_loop(1, CHIPS, start_chunk, 0)
    own = pltpu.make_async_copy(out_ref.at[tok * 2 + y // 2], recv_ref.at[0, 0], local.at[0])
    own.start()
    own_page = pltpu.make_async_copy(pages_ref.at[tok], arrived_ref.at[tok], local.at[1])
    own_page.start()
    lax.fori_loop(1, 16, start_page, 0)
    own.wait()

    def forward(g):
        block = pl.ds(g * 8, 8)
        return remote(recv_ref.at[0, block], recv_ref.at[1, block], fsend.at[g], frecv.at[g], sib)

    def arrive(k, carry):
        chunk(k).wait_recv()
        return carry

    def pass_on(g, carry):
        lax.fori_loop(jnp.maximum(g * 8, 1), g * 8 + 8, arrive, 0)
        forward(g).start()
        return carry

    lax.fori_loop(0, 8, pass_on, 0)

    def finish_forward(g, carry):
        forward(g).wait()
        return carry

    def finish_chunk(k, carry):
        chunk(k).wait_send()
        return carry

    def finish_page(j, carry):
        page(j).wait()
        return carry

    lax.fori_loop(0, 8, finish_forward, 0)
    lax.fori_loop(1, CHIPS, finish_chunk, 0)
    lax.fori_loop(1, 16, finish_page, 0)
    own_page.wait()


def dispatch(outgoing, pages):
    return pl.pallas_call(
        dispatch_kernel,
        out_shape=(
            jax.ShapeDtypeStruct((2, CHIPS, CHUNK, PART_WIDTH), jnp.bfloat16),
            jax.ShapeDtypeStruct((16, PAGE_TOKENS, 2 * HEAD_SIZE), jnp.bfloat16),
        ),
        in_specs=[vmem_spec(), vmem_spec()],
        out_specs=(any_spec(), any_spec()),
        scratch_shapes=[
            pltpu.SemaphoreType.DMA((CHIPS,)),
            pltpu.SemaphoreType.DMA((CHIPS,)),
            pltpu.SemaphoreType.DMA((8,)),
            pltpu.SemaphoreType.DMA((8,)),
            pltpu.SemaphoreType.DMA((16,)),
            pltpu.SemaphoreType.DMA((16,)),
            pltpu.SemaphoreType.DMA((2,)),
        ],
        compiler_params=pltpu.CompilerParams(collective_id=2, has_side_effects=True),
        name="dispatch",
    )(outgoing, pages)


GROUPS = 8
GROUP_ROWS = 2 * CHIPS * CHUNK // GROUPS
GROUP_SLOTS = GROUP_ROWS // PARTS
EXPERT_ROWS = GROUPS * GROUP_SLOTS
DOT_ROWS = 256


def expert_kernel(recv_ref, win_ref, wdown_ref, y_ref, rbuf, w1, w2, xs, acc, ys, sem):
    copies_r = [
        pltpu.make_async_copy(recv_ref.at[b], rbuf.at[b], sem.at[b]) for b in range(GROUPS)
    ]
    copies_w = [
        pltpu.make_async_copy(
            win_ref.at[pl.ds(q * PART_WIDTH, PART_WIDTH)], w1.at[q], sem.at[GROUPS + q]
        )
        for q in range(PARTS)
    ]
    copy_d = pltpu.make_async_copy(wdown_ref, w2, sem.at[GROUPS + PARTS])
    for copy in copies_r + copies_w + [copy_d]:
        copy.start()
    shape = (GROUP_ROWS, GROUP_ROWS)
    part, row = split_index(iota(shape, 0), GROUP_SLOTS)
    row_source, row_slot = split_index(row, SLOTS)
    col_source, col = split_index(iota(shape, 1), CHUNK)
    col_part, col_slot = split_index(col, SLOTS)
    match = (part == col_part) & (row_source == col_source) & (row_slot == col_slot)
    perm = jnp.where(match, 1.0, 0.0).astype(jnp.bfloat16)
    part, row = split_index(iota(shape, 1), GROUP_SLOTS)
    row_source, row_slot = split_index(row, SLOTS)
    col_source, col = split_index(iota(shape, 0), CHUNK)
    col_part, col_slot = split_index(col, SLOTS)
    match = (part == col_part) & (row_source == col_source) & (row_slot == col_slot)
    back = jnp.where(match, 1.0, 0.0).astype(jnp.bfloat16)
    for copy in copies_r:
        copy.wait()

    def sort_in(b, carry):
        mixed = jnp.dot(perm, rbuf[b], preferred_element_type=jnp.float32).astype(jnp.bfloat16)
        start = pl.multiple_of(b * GROUP_SLOTS, GROUP_SLOTS)
        for q in range(PARTS):
            xs[q, pl.ds(start, GROUP_SLOTS), :] = mixed[q * GROUP_SLOTS : (q + 1) * GROUP_SLOTS]
        return carry

    lax.fori_loop(0, GROUPS, sort_in, 0)
    for copy in copies_w:
        copy.wait()

    def up_block(i, carry):
        rows = pl.ds(pl.multiple_of(i * DOT_ROWS, DOT_ROWS), DOT_ROWS)
        acc[...] = jnp.dot(xs[0, rows, :], w1[0], preferred_element_type=jnp.float32)
        for q in range(1, PARTS):
            acc[...] += jnp.dot(xs[q, rows, :], w1[q], preferred_element_type=jnp.float32)
        gate = acc[:, :PART_WIDTH]
        up = acc[:, PART_WIDTH:]
        act = (up + 1.0) * gate * jax.nn.sigmoid(GLU_ALPHA * gate)
        xs[0, rows, :] = act.astype(jnp.bfloat16)
        return carry

    lax.fori_loop(0, EXPERT_ROWS // DOT_ROWS, up_block, 0)
    copy_d.wait()

    def down_block(i, carry):
        rows = pl.ds(pl.multiple_of(i * DOT_ROWS, DOT_ROWS), DOT_ROWS)
        down = jnp.dot(xs[0, rows, :], w2[...], preferred_element_type=jnp.float32)
        down = down.astype(jnp.bfloat16)
        for q in range(PARTS):
            ys[q, rows, :] = down[:, q * PART_WIDTH : (q + 1) * PART_WIDTH]
        return carry

    lax.fori_loop(0, EXPERT_ROWS // DOT_ROWS, down_block, 0)

    def sort_out(b, carry):
        rows = pl.ds(pl.multiple_of(b * GROUP_SLOTS, GROUP_SLOTS), GROUP_SLOTS)
        total = jnp.zeros((GROUP_ROWS, PART_WIDTH), jnp.float32)
        stacked = jnp.concatenate([ys[q, rows, :] for q in range(PARTS)], axis=0)
        y_ref[b] = jnp.dot(back, stacked, preferred_element_type=jnp.float32).astype(jnp.bfloat16)
        return carry

    lax.fori_loop(0, GROUPS, sort_out, 0)


def run_experts(received, w_in, w_down):
    out = pl.pallas_call(
        expert_kernel,
        out_shape=jax.ShapeDtypeStruct((GROUPS, GROUP_ROWS, PART_WIDTH), jnp.bfloat16),
        in_specs=[any_spec()] * 3,
        out_specs=vmem_spec(),
        scratch_shapes=[
            VM((GROUPS, GROUP_ROWS, PART_WIDTH), jnp.bfloat16),
            VM((PARTS, PART_WIDTH, 2 * PART_WIDTH), jnp.bfloat16),
            VM((PART_WIDTH, MODEL_WIDTH), jnp.bfloat16),
            VM((PARTS, EXPERT_ROWS, PART_WIDTH), jnp.bfloat16),
            VM((DOT_ROWS, 2 * PART_WIDTH), jnp.float32),
            VM((PARTS, EXPERT_ROWS, PART_WIDTH), jnp.bfloat16),
            pltpu.SemaphoreType.DMA((GROUPS + PARTS + 1,)),
        ],
        compiler_params=pltpu.CompilerParams(vmem_limit_bytes=60 << 20),
        name="run_experts",
    )(received.reshape(GROUPS, GROUP_ROWS, PART_WIDTH), w_in, w_down)
    return out.reshape(2, CHIPS, CHUNK, PART_WIDTH)


def return_kernel(y_ref, ret_ref, own, pair, sums, psend, precv, send, recv, lsem, last):
    barrier = pltpu.get_barrier_semaphore()
    sib = sibling()
    greet_all(barrier)

    def load(g):
        block = pl.ds(g * 8, 8)
        return pltpu.make_async_copy(y_ref.at[0, block], own.at[block], lsem.at[g])

    def start_load(g, carry):
        load(g).start()
        return carry

    lax.fori_loop(0, 8, start_load, 0)
    pl.semaphore_wait(barrier, CHIPS)

    def exchange(g):
        block = pl.ds(g * 8, 8)
        return remote(y_ref.at[1, block], pair.at[block], psend.at[g], precv.at[g], sib)

    def start_exchange(g, carry):
        exchange(g).start()
        return carry

    lax.fori_loop(0, 8, start_exchange, 0)

    def chunk(k):
        return remote(
            sums.at[k], ret_ref.at[k], send.at[k], recv.at[k], device(*shifted(k, -1))
        )

    def start_chunk(k, carry):
        chunk(k).start()
        return carry

    def add(g, carry):
        exchange(g).wait_recv()
        load(g).wait()
        block = pl.ds(g * 8, 8)
        sums[block] = (own[block].astype(jnp.float32) + pair[block].astype(jnp.float32)).astype(
            jnp.bfloat16
        )
        lax.fori_loop(jnp.maximum((g - 1) * 8, 1), g * 8, start_chunk, 0)
        return carry

    lax.fori_loop(0, 8, add, 0)
    home = pltpu.make_async_copy(sums.at[0], ret_ref.at[0], last)
    home.start()
    lax.fori_loop(CHIPS - 8, CHIPS, start_chunk, 0)

    def finish_exchange(g, carry):
        exchange(g).wait_send()
        return carry

    def finish_chunk(k, carry):
        chunk(k).wait()
        return carry

    lax.fori_loop(0, 8, finish_exchange, 0)
    lax.fori_loop(1, CHIPS, finish_chunk, 0)
    home.wait()


def give_back(y):
    return pl.pallas_call(
        return_kernel,
        out_shape=jax.ShapeDtypeStruct((CHIPS, CHUNK, PART_WIDTH), jnp.bfloat16),
        in_specs=[any_spec()],
        out_specs=any_spec(),
        scratch_shapes=[
            VM((CHIPS, CHUNK, PART_WIDTH), jnp.bfloat16),
            VM((CHIPS, CHUNK, PART_WIDTH), jnp.bfloat16),
            VM((CHIPS, CHUNK, PART_WIDTH), jnp.bfloat16),
            pltpu.SemaphoreType.DMA((8,)),
            pltpu.SemaphoreType.DMA((8,)),
            pltpu.SemaphoreType.DMA((CHIPS,)),
            pltpu.SemaphoreType.DMA((CHIPS,)),
            pltpu.SemaphoreType.DMA((8,)),
            pltpu.SemaphoreType.DMA,
        ],
        compiler_params=pltpu.CompilerParams(collective_id=3, has_side_effects=True),
        name="give_back",
    )(y)


def combine_kernel(ret_ref, resid_ref, routes_ref, gates_ref, live_ref, home_ref, out_ref):
    expert = iota((ROWS, EXPERTS), 1)
    routed = jnp.zeros((ROWS, EXPERTS), jnp.float32)
    gate = jnp.zeros((ROWS, EXPERTS), jnp.float32)
    for k in range(4):
        named = routes_ref[:, k : k + 1] == expert
        routed = routed + jnp.where(named, 1.0, 0.0)
        gate = gate + jnp.where(named, gates_ref[:, k : k + 1], 0.0)
    routed = routed * live_ref[0:1, :EXPERTS]
    earlier = jnp.where(iota((ROWS, ROWS), 1) < iota((ROWS, ROWS), 0), 1.0, 0.0)
    rank = jnp.dot(
        earlier.astype(jnp.bfloat16), routed.astype(jnp.bfloat16), preferred_element_type=jnp.float32
    )
    code = jnp.where(routed > 0.5, rank, -1.0).astype(jnp.bfloat16)
    count = CHIPS * CHUNK
    spread = jnp.where(iota((EXPERTS, count), 0) == home_ref[...], 1.0, 0.0).astype(jnp.bfloat16)
    code_cols = jnp.dot(code, spread, preferred_element_type=jnp.float32)
    gate_cols = jnp.dot(gate.astype(jnp.bfloat16), spread, preferred_element_type=jnp.float32)
    _, within = split_index(iota((ROWS, count), 1), CHUNK)
    part, slot = split_index(within, SLOTS)
    weight = jnp.where(jnp.abs(code_cols - slot.astype(jnp.float32)) < 0.5, gate_cols, 0.0)
    stacked = jnp.concatenate(
        [jnp.where(part == q, weight, 0.0).astype(jnp.bfloat16) for q in range(PARTS)], axis=0
    )
    total = jnp.dot(stacked, ret_ref[...], preferred_element_type=jnp.float32)
    for q in range(PARTS):
        cols = slice(q * PART_WIDTH, (q + 1) * PART_WIDTH)
        out_ref[:, cols] = (
            resid_ref[:, cols] + total[q * ROWS : (q + 1) * ROWS]
        ).astype(jnp.bfloat16)


def combine(returned, resid, routes, gates, live_row):
    x, y, z, _ = place()
    k = jnp.arange(CHIPS * CHUNK, dtype=jnp.int32)[None, :] // CHUNK
    home = (((x + k // 16) % 4) * 4 + (z + k % 4) % 4) * 2 + ((y + (k // 4) % 4) % 4) // 2
    return pl.pallas_call(
        combine_kernel,
        out_shape=jax.ShapeDtypeStruct((ROWS, MODEL_WIDTH), jnp.bfloat16),
        in_specs=[vmem_spec()] * 6,
        out_specs=vmem_spec(),
        name="combine",
    )(returned.reshape(CHIPS * CHUNK, PART_WIDTH), resid, routes, gates, live_row, home)


def page_order(page_table, n_tok, pages_dev):
    page_grid = page_table.reshape(n_tok, pages_dev)
    target = page_grid // pages_dev
    page_ids = jnp.arange(pages_dev, dtype=jnp.int32)
    earlier = page_ids[:, None] > page_ids[None, :]
    same_dest = target[:, :, None] == target[:, None, :]
    order_rank = jnp.sum((same_dest & earlier[None]).astype(jnp.int32), axis=2)
    return (target, order_rank, page_grid % pages_dev)


def per_device(
    tokens,
    lengths,
    norm_gain_attn,
    query_key_value_weight,
    sinks,
    w_out_attn,
    norm_gain_moe,
    routes,
    gates,
    w_in,
    w_down,
    page_table,
):
    n_tok = lax.axis_size("tok")
    n_head = lax.axis_size("head")
    tok_id = lax.axis_index("tok")
    head_id = lax.axis_index("head")
    row_count = tokens.shape[0]
    tok_dev = row_count * n_head
    groups = sinks.shape[0] // QUERY_PER_KEY
    normed_input = normalize(tokens, norm_gain_attn).astype(jnp.bfloat16)
    projected_rows = jnp.dot(
        gather_rows(normed_input),
        query_key_value_weight,
        preferred_element_type=jnp.float32,
    ).reshape(tok_dev, groups, QUERY_PER_KEY + 2, HEAD_SIZE)
    row_base = tok_id * tok_dev
    query_index = row_base + jnp.arange(tok_dev, dtype=jnp.int32)
    query_segs, positions = segment_table(lengths, query_index)
    query_rows = (
        rotate(projected_rows[:, :, :QUERY_PER_KEY], positions) * HEAD_SIZE ** (-0.5)
    ).astype(jnp.bfloat16)
    key_rot = rotate(projected_rows[:, :, QUERY_PER_KEY], positions)
    key_value_pairs = jnp.concatenate(
        [key_rot, projected_rows[:, :, QUERY_PER_KEY + 1]], axis=-1
    ).astype(jnp.bfloat16)
    rim_rows = passed_along(key_value_pairs[tok_dev - ATTEND_WINDOW :], "tok", 1)
    key_index = row_base - ATTEND_WINDOW + jnp.arange(tok_dev + ATTEND_WINDOW, dtype=jnp.int32)
    key_segs, _ = segment_table(lengths, key_index)
    allowed = band_mask(query_index, key_index, query_segs, key_segs, ATTEND_WINDOW)
    attended = band_attention(
        query_rows,
        jnp.concatenate([rim_rows, key_value_pairs], axis=0),
        sinks.reshape(groups, QUERY_PER_KEY),
        allowed,
    )
    attn_sum = sum_over_heads(
        jnp.dot(attended, w_out_attn, preferred_element_type=jnp.float32).astype(jnp.bfloat16)
    )
    live = jnp.where((tok_id * n_head + head_id) * row_count < jnp.sum(lengths), 1.0, 0.0)
    live_row = jnp.full((1, 128), live, jnp.float32)
    resid, outgoing = prepare_chunks(attn_sum, tokens, norm_gain_moe, jnp.transpose(routes), live_row)
    pages_dev = tok_dev // PAGE_TOKENS
    share_count = pages_dev // n_tok
    paged = key_value_pairs.reshape(pages_dev, PAGE_TOKENS, groups, 2 * HEAD_SIZE)
    target, order_rank, slot_grid = page_order(page_table, n_tok, pages_dev)
    dest_ids = jnp.arange(n_tok, dtype=jnp.int32)
    share_ids = jnp.arange(share_count, dtype=jnp.int32)
    page_ids = jnp.arange(pages_dev, dtype=jnp.int32)
    my_target = target[tok_id]
    my_rank = order_rank[tok_id]
    matched = (my_target[:, None, None] == dest_ids[None, :, None]) & (
        my_rank[:, None, None] == share_ids[None, None, :]
    )
    pick_page = jnp.sum(jnp.where(matched, page_ids[:, None, None], 0), axis=0)
    received, arrived = dispatch(outgoing, paged[pick_page].reshape(n_tok, PAGE_TOKENS, 2 * HEAD_SIZE))
    returned = give_back(run_experts(received, w_in[0], w_down[0]))
    hidden_out = combine(returned, resid, routes, gates, live_row)
    to_here = (target == tok_id)[:, :, None] & (order_rank[:, :, None] == share_ids[None, None, :])
    landing = jnp.sum(jnp.where(to_here, slot_grid[:, :, None], 0), axis=1)
    stored = jnp.zeros_like(paged).at[landing.reshape(-1)].set(arrived.reshape(paged.shape))
    kv_cache = jnp.transpose(stored, (2, 0, 1, 3))
    return (hidden_out, kv_cache)


def solution(mesh):
    return jax.shard_map(
        per_device,
        mesh=mesh,
        in_specs=(
            P(("tok", "head"), None),
            P(),
            P(),
            P(None, "head"),
            P("head"),
            P("head", None),
            P(),
            P(("tok", "head"), None),
            P(("tok", "head"), None),
            P(("tok", "head"), None, None),
            P(("tok", "head"), None, None),
            P(),
        ),
        out_specs=(P(("tok", "head"), None), P("head", "tok", None, None)),
        check_vma=False,
    )
```

```python
import math

import jax
import jax.numpy as jnp
import numpy as np
from jax import lax
from jax.experimental import pallas as pl
from jax.experimental.pallas import tpu as pltpu
from jax.sharding import PartitionSpec as P

MODEL_WIDTH = 2880
HEAD_SIZE = 64
EXPERTS = 32
ATTEND_WINDOW = 128
PAGE_TOKENS = 16
QUERY_PER_KEY = 8

EPSILON = 1e-05
ROPE_BASE = 150000.0
GLU_ALPHA = 1.702

MESH = pl.DeviceIdType.MESH
VM = pltpu.VMEM
CHIPS = 64
ROWS = 32
SLOTS = 6
PARTS = 4
PART_WIDTH = MODEL_WIDTH // PARTS
CHUNK = PARTS * SLOTS
HEADS = 8


def vmem_spec():
    return pl.BlockSpec(memory_space=pltpu.VMEM)


def any_spec():
    return pl.BlockSpec(memory_space=pl.ANY)


def place():
    tok = lax.axis_index("tok")
    head = lax.axis_index("head")
    return (tok // 4, head // 2, tok % 4, head % 2)


def device(x, y, z, core):
    return (x * 4 + z, y * 2 + core)


def shifted(k, sign):
    x, y, z, core = place()
    dx, dy, dz = k // 16, (k // 4) % 4, k % 4
    if sign < 0:
        dx, dy, dz = 4 - dx, 4 - dy, 4 - dz
    return ((x + dx) % 4, (y + dy) % 4, (z + dz) % 4, core)


def sibling():
    x, y, z, core = place()
    return device(x, y, z, 1 - core)


def signal(barrier, target):
    pl.semaphore_signal(barrier, inc=1, device_id=target, device_id_type=MESH)

def far_first():
    def steps(k):
        return sum(min(d, 4 - d) for d in (k // 16, (k // 4) % 4, k % 4))

    return sorted(range(CHIPS), key=lambda k: -steps(k))


ORDER = far_first()


def greet_all(barrier):
    def greet(k, carry):
        signal(barrier, device(*shifted(k, 1)))
        return carry

    lax.fori_loop(1, CHIPS, greet, 0)
    signal(barrier, sibling())


def remote(src, dst, send, recv, target):
    return pltpu.make_async_remote_copy(
        src_ref=src, dst_ref=dst, send_sem=send, recv_sem=recv, device_id=target, device_id_type=MESH
    )


def iota(shape, dim):
    return lax.broadcasted_iota(jnp.int32, shape, dim)


def split_index(index, size):
    whole = jnp.floor((index.astype(jnp.float32) + 0.5) * (1.0 / size)).astype(jnp.int32)
    return (whole, index - whole * size)


TOK_ROWS = HEADS * ROWS
QKV = (QUERY_PER_KEY + 2) * HEAD_SIZE
LANES = 2 * HEAD_SIZE
HEAD_COLS = QUERY_PER_KEY * HEAD_SIZE
TOKS = 16


def swap_halves(values, lane):
    half = HEAD_SIZE // 2
    ahead = pltpu.roll(values, LANES - half, 1)
    behind = pltpu.roll(values, half, 1)
    return jnp.where(lane < half, ahead, behind)


def sequence_start(index, len_ref):
    start = jnp.zeros_like(index)
    end = jnp.int32(0)
    for s in range(4):
        end = end + len_ref[s]
        start = start + jnp.where(index >= end, len_ref[s], 0)
    return start, end


def expert_code(routes_ref, live):
    expert = iota((EXPERTS, ROWS), 0)
    routed = jnp.zeros((EXPERTS, ROWS), jnp.float32)
    for k in range(4):
        routed = routed + jnp.where(routes_ref[k : k + 1, :] == expert, 1.0, 0.0)
    routed = routed * live
    earlier = jnp.where(iota((ROWS, ROWS), 0) < iota((ROWS, ROWS), 1), 1.0, 0.0)
    rank = jnp.dot(
        routed.astype(jnp.bfloat16), earlier.astype(jnp.bfloat16), preferred_element_type=jnp.float32
    )
    return jnp.where(routed > 0.5, rank, -1.0).astype(jnp.bfloat16)


def block_live(len_ref, tok, head):
    total = len_ref[0] + len_ref[1] + len_ref[2] + len_ref[3]
    index = iota((EXPERTS, ROWS), 1) + (tok * TOK_ROWS + head * ROWS)
    return jnp.where(index < total, 1.0, 0.0)


def front_kernel(
    tok_ref,
    gain_attn_ref,
    gain_moe_ref,
    len_ref,
    routes_ref,
    table_ref,
    sinks_ref,
    wqkv_ref,
    wout_ref,
    resid_ref,
    recv_ref,
    arrived_ref,
    xn,
    wq,
    wo,
    halo,
    kvs,
    att,
    part,
    pair,
    sums,
    far,
    outg,
    pages,
    wsem,
    asend,
    arecv,
    fsend,
    frecv,
    hsem,
    psend,
    precv,
    rsend,
    rrecv,
    gsend,
    grecv,
    csend,
    crecv,
    bsend,
    brecv,
    local,
):
    x, y, z, core = place()
    tok = x * 4 + z
    head = y * 2 + core
    sib = sibling()
    barrier = pltpu.get_barrier_semaphore()
    greet_all(barrier)
    load_q = pltpu.make_async_copy(wqkv_ref, wq, wsem.at[0])
    load_o = pltpu.make_async_copy(wout_ref, wo, wsem.at[1])
    load_q.start()
    load_o.start()

    mine = y * 2 + core
    lower = ((y + 3) % 4) * 2 + core
    upper = ((y + 1) % 4) * 2 + core
    opposite = ((y + 2) % 4) * 2 + core
    wide = tok_ref[...].astype(jnp.float32)
    inv_rms = lax.rsqrt(jnp.mean(wide * wide, axis=-1, keepdims=True) + EPSILON)
    xn[mine] = (wide * inv_rms * gain_attn_ref[...]).astype(jnp.bfloat16)
    pl.semaphore_wait(barrier, CHIPS)

    up = device(x, (y + 1) % 4, z, core)
    down = device(x, (y + 3) % 4, z, core)
    half = ROWS // 2
    first = pl.ds(0, half)
    second = pl.ds(half, half)
    to_up = remote(xn.at[mine], xn.at[mine], asend.at[0], arecv.at[0], up)
    to_down = remote(xn.at[mine], xn.at[mine], asend.at[1], arecv.at[1], down)
    to_sib = remote(xn.at[mine], xn.at[mine], fsend.at[0], frecv.at[0], sib)
    to_up.start()
    to_down.start()
    to_sib.start()

    lane = iota((TOK_ROWS, LANES), 1)
    lane64 = jnp.where(lane < HEAD_SIZE, lane, lane - HEAD_SIZE)
    lane32 = jnp.where(lane64 < HEAD_SIZE // 2, lane64, lane64 - HEAD_SIZE // 2)
    index = iota((TOK_ROWS, LANES), 0) + tok * TOK_ROWS
    start, total = sequence_start(index, len_ref)
    rate = jnp.exp(lane32.astype(jnp.float32) * (-2.0 * math.log(ROPE_BASE) / HEAD_SIZE))
    angle = (index - start).astype(jnp.float32) * rate
    cos_table = jnp.cos(angle)
    sin_table = jnp.where(lane64 < HEAD_SIZE // 2, -jnp.sin(angle), jnp.sin(angle))

    to_up.wait_recv()
    on_up = remote(xn.at[lower, first], xn.at[lower, first], asend.at[2], arecv.at[2], up)
    on_up.start()
    sib_low = remote(xn.at[lower], xn.at[lower], fsend.at[1], frecv.at[1], sib)
    sib_low.start()
    to_down.wait_recv()
    on_down = remote(xn.at[upper, second], xn.at[upper, second], asend.at[3], arecv.at[3], down)
    on_down.start()
    sib_up = remote(xn.at[upper], xn.at[upper], fsend.at[2], frecv.at[2], sib)
    sib_up.start()
    on_up.wait_recv()
    on_down.wait_recv()
    sib_far = remote(xn.at[opposite], xn.at[opposite], fsend.at[3], frecv.at[3], sib)
    sib_far.start()
    for copy in (to_sib, sib_low, sib_up, sib_far):
        copy.wait_recv()
    load_q.wait()

    projected = jnp.dot(
        xn[...].reshape(TOK_ROWS, MODEL_WIDTH), wq[...], preferred_element_type=jnp.float32
    )

    slab = projected[:, HEAD_COLS:]
    turned = slab * cos_table + swap_halves(slab, lane64) * sin_table
    kvs[...] = jnp.where(lane < HEAD_SIZE, turned, slab).astype(jnp.bfloat16)
    after = (tok + 1) % TOKS
    to_next = remote(
        kvs.at[pl.ds(TOK_ROWS - ATTEND_WINDOW, ATTEND_WINDOW)],
        halo,
        hsem.at[0],
        hsem.at[1],
        (after, head),
    )
    to_next.start()
    queries = []
    for s in range(HEAD_COLS // LANES):
        slab = projected[:, s * LANES : (s + 1) * LANES]
        turned = slab * cos_table + swap_halves(slab, lane64) * sin_table
        queries.append(turned * HEAD_SIZE ** (-0.5))

    row_page, row_in = split_index(iota((TOK_ROWS, TOK_ROWS), 0), PAGE_TOKENS)
    col_page, col_in = split_index(iota((TOK_ROWS, TOK_ROWS), 1), PAGE_TOKENS)
    col_of = split_index(iota((1, TOK_ROWS), 1), PAGE_TOKENS)[0]
    target = jnp.zeros((1, TOK_ROWS), jnp.int32)
    for p in range(TOKS):
        target = target + jnp.where(col_of == p, table_ref[tok * TOKS + p] // TOKS, 0)
    pick = jnp.where((target == row_page) & (row_in == col_in), 1.0, 0.0).astype(jnp.bfloat16)
    sorted_rows = jnp.dot(pick, kvs[...], preferred_element_type=jnp.float32).astype(jnp.bfloat16)
    pages[...] = sorted_rows.reshape(TOKS, PAGE_TOKENS, LANES)

    def page(j):
        tx, tz = (x + j // 4) % 4, (z + j % 4) % 4
        return remote(
            pages.at[tx * 4 + tz], arrived_ref.at[tok], gsend.at[j], grecv.at[j], device(tx, y, tz, core)
        )

    def attend(b):
        wide_halo = halo[...].astype(jnp.float32)
        wide_kv = kvs[...].astype(jnp.float32)
        if b == 0:
            before = jnp.where(tok * jnp.ones_like(wide_halo) > 0.5, wide_halo, 0.0)
            band = jnp.concatenate([before, wide_kv[:ATTEND_WINDOW]], axis=0)
        else:
            band = wide_kv
        turned = pltpu.roll(band, HEAD_SIZE, 1)
        lanes = iota((2 * ATTEND_WINDOW, LANES), 1)
        keys = jnp.where(lanes < HEAD_SIZE, band, turned).astype(jnp.bfloat16)
        values = jnp.where(lanes < HEAD_SIZE, turned, band).astype(jnp.bfloat16)
        lo = iota((ATTEND_WINDOW, LANES), 1) < HEAD_SIZE
        stack = []
        for s in range(HEAD_COLS // LANES):
            rows = queries[s][b * ATTEND_WINDOW : (b + 1) * ATTEND_WINDOW]
            stack.append(jnp.where(lo, rows, 0.0).astype(jnp.bfloat16))
            stack.append(jnp.where(lo, 0.0, rows).astype(jnp.bfloat16))
        scores = lax.dot_general(
            jnp.concatenate(stack, axis=0),
            keys,
            (((1,), (1,)), ((), ())),
            preferred_element_type=jnp.float32,
        )
        shape = (ATTEND_WINDOW, 2 * ATTEND_WINDOW)
        query = iota(shape, 0) + (tok * TOK_ROWS + b * ATTEND_WINDOW)
        began, ends = sequence_start(query, len_ref)
        distance = iota(shape, 0) + ATTEND_WINDOW - iota(shape, 1)
        reach = jnp.minimum(query - began, ATTEND_WINDOW - 1)
        allowed = (distance >= 0) & (distance <= reach) & (query < ends)
        sink = jnp.exp(sinks_ref[...])
        probs = []
        for n in range(QUERY_PER_KEY):
            block = scores[n * ATTEND_WINDOW : (n + 1) * ATTEND_WINDOW]
            weights = jnp.where(allowed, jnp.exp(block), 0.0)
            totals = jnp.sum(weights, axis=-1, keepdims=True) + sink[0:1, n : n + 1]
            probs.append((weights / totals).astype(jnp.bfloat16))
        mixed = jnp.dot(
            jnp.concatenate(probs, axis=0), values, preferred_element_type=jnp.float32
        )
        for s in range(HEAD_COLS // LANES):
            even = mixed[2 * s * ATTEND_WINDOW : (2 * s + 1) * ATTEND_WINDOW]
            odd = mixed[(2 * s + 1) * ATTEND_WINDOW : (2 * s + 2) * ATTEND_WINDOW]
            both = jnp.where(lo, even, odd).astype(jnp.bfloat16)
            att[b * 4 : (b + 1) * 4, :, s * LANES : (s + 1) * LANES] = both.reshape(4, ROWS, LANES)

    def start_page(j, carry):
        page(j).start()
        return carry

    own_page = pltpu.make_async_copy(pages.at[tok], arrived_ref.at[tok], local.at[1])
    attend(1)
    lax.fori_loop(1, TOKS, start_page, 0)
    own_page.start()
    to_next.wait_recv()
    attend(0)
    load_o.wait()

    owners = [(y + 1) % 4, (y + 2) % 4, (y + 3) % 4, y]
    contract = (((1,), (1,)), ((), ()))
    rows = jnp.concatenate([att[o * 2 + 1 - core] for o in owners], axis=0)
    theirs = lax.dot_general(rows, wo[...], contract, preferred_element_type=jnp.float32)
    part[...] = theirs.astype(jnp.bfloat16).reshape(4, ROWS, MODEL_WIDTH)
    pairs = []
    for i in range(4):
        copy = remote(part.at[i], pair.at[i], psend.at[i], precv.at[i], sib)
        copy.start()
        pairs.append(copy)
    rows = jnp.concatenate([att[o * 2 + core] for o in owners], axis=0)
    ours = lax.dot_general(rows, wo[...], contract, preferred_element_type=jnp.float32)
    sent = []
    for i in range(4):
        pairs[i].wait_recv()
        both = ours[i * ROWS : (i + 1) * ROWS] + pair[i].astype(jnp.float32)
        if i < 3:
            sums[i] = both.astype(jnp.bfloat16)
        if i > 0:
            copy = remote(
                sums.at[i - 1], far.at[i - 1], rsend.at[i - 1], rrecv.at[i - 1], device(x, owners[i - 1], z, core)
            )
            copy.start()
            sent.append(copy)

    code = expert_code(routes_ref, block_live(len_ref, tok, head))
    count = EXPERTS * CHUNK
    owner, _ = split_index(iota((count, EXPERTS), 0), CHUNK)
    spread = jnp.where(owner == iota((count, EXPERTS), 1), 1.0, 0.0).astype(jnp.bfloat16)
    code_rows = jnp.dot(spread, code, preferred_element_type=jnp.float32)
    _, within = split_index(iota((count, ROWS), 0), CHUNK)
    quarter, slot = split_index(within, SLOTS)
    hit = jnp.abs(code_rows - slot.astype(jnp.float32)) < 0.5
    picks = [
        jnp.where(hit & (quarter == q), 1.0, 0.0).astype(jnp.bfloat16) for q in range(PARTS)
    ]

    resid = tok_ref[...].astype(jnp.float32) + both
    for i in range(3):
        sent[i].wait_recv()
        resid = resid + far[i].astype(jnp.float32)
    resid_ref[...] = resid
    inv_rms = lax.rsqrt(jnp.mean(resid * resid, axis=-1, keepdims=True) + EPSILON)
    moe_in = (resid * inv_rms * gain_moe_ref[...]).astype(jnp.bfloat16)
    chunks = jnp.zeros((count, PART_WIDTH), jnp.float32)
    for q in range(PARTS):
        chunks = chunks + jnp.dot(
            picks[q],
            moe_in[:, q * PART_WIDTH : (q + 1) * PART_WIDTH],
            preferred_element_type=jnp.float32,
        )
    outg[...] = chunks.reshape(EXPERTS, CHUNK, PART_WIDTH).astype(jnp.bfloat16)

    for i in range(CHIPS - 1):
        tx, ty, tz, tc = shifted(ORDER[i], 1)
        expert = (tx * 4 + tz) * 2 + ty // 2
        remote(
            outg.at[expert], recv_ref.at[0, i], csend.at[i], crecv.at[i], device(tx, ty, tz, tc)
        ).start()
    own = pltpu.make_async_copy(outg.at[tok * 2 + y // 2], recv_ref.at[0, CHIPS - 1], local.at[0])
    own.start()

    def received(i):
        return remote(outg.at[0], recv_ref.at[0, i], csend.at[i], crecv.at[i], sib)

    def forward(g):
        block = pl.ds(g * 8, 8)
        return remote(recv_ref.at[0, block], recv_ref.at[1, block], bsend.at[g], brecv.at[g], sib)

    def arrive(i, carry):
        received(i).wait_recv()
        return carry

    def pass_on(g, carry):
        lax.fori_loop(g * 8, g * 8 + 8, arrive, 0)
        forward(g).start()
        return carry

    lax.fori_loop(0, 7, pass_on, 0)
    own.wait()
    lax.fori_loop(CHIPS - 8, CHIPS - 1, arrive, 0)
    forward(7).start()

    def finish_forward(g, carry):
        forward(g).wait()
        return carry

    def finish_chunk(i, carry):
        received(i).wait_send()
        return carry

    def finish_page(j, carry):
        page(j).wait()
        return carry

    lax.fori_loop(0, 8, finish_forward, 0)
    lax.fori_loop(0, CHIPS - 1, finish_chunk, 0)
    lax.fori_loop(1, TOKS, finish_page, 0)
    own_page.wait()
    for copy in pairs + sent + [to_up, to_down, on_up, on_down, to_sib, sib_low, sib_up, sib_far]:
        copy.wait_send()
    to_next.wait_send()


def front(tokens, gain_attn, gain_moe, lengths, routes_t, page_table, sinks, w_qkv, w_out_t):
    bf, dma = jnp.bfloat16, pltpu.SemaphoreType.DMA
    smem = pl.BlockSpec(memory_space=pltpu.SMEM)
    return pl.pallas_call(
        front_kernel,
        out_shape=(
            jax.ShapeDtypeStruct((ROWS, MODEL_WIDTH), jnp.float32),
            jax.ShapeDtypeStruct((2, CHIPS, CHUNK, PART_WIDTH), bf),
            jax.ShapeDtypeStruct((TOKS, PAGE_TOKENS, LANES), bf),
        ),
        in_specs=[
            vmem_spec(),
            vmem_spec(),
            vmem_spec(),
            smem,
            vmem_spec(),
            smem,
            vmem_spec(),
            any_spec(),
            any_spec(),
        ],
        out_specs=(vmem_spec(), any_spec(), any_spec()),
        scratch_shapes=[
            VM((HEADS, ROWS, MODEL_WIDTH), bf),
            VM((MODEL_WIDTH, QKV), bf),
            VM((MODEL_WIDTH, HEAD_COLS), bf),
            VM((ATTEND_WINDOW, LANES), bf),
            VM((TOK_ROWS, LANES), bf),
            VM((HEADS, ROWS, HEAD_COLS), bf),
            VM((4, ROWS, MODEL_WIDTH), bf),
            VM((4, ROWS, MODEL_WIDTH), bf),
            VM((3, ROWS, MODEL_WIDTH), bf),
            VM((3, ROWS, MODEL_WIDTH), bf),
            VM((EXPERTS, CHUNK, PART_WIDTH), bf),
            VM((TOKS, PAGE_TOKENS, LANES), bf),
            dma((2,)),
            dma((4,)),
            dma((4,)),
            dma((4,)),
            dma((4,)),
            dma((2,)),
            dma((4,)),
            dma((4,)),
            dma((3,)),
            dma((3,)),
            dma((TOKS,)),
            dma((TOKS,)),
            dma((CHIPS,)),
            dma((CHIPS,)),
            dma((8,)),
            dma((8,)),
            dma((2,)),
        ],
        compiler_params=pltpu.CompilerParams(
            collective_id=0, has_side_effects=True, vmem_limit_bytes=60 << 20
        ),
        name="front",
    )(
        tokens,
        gain_attn.reshape(1, MODEL_WIDTH),
        gain_moe.reshape(1, MODEL_WIDTH),
        lengths,
        routes_t,
        page_table,
        sinks.reshape(1, QUERY_PER_KEY),
        w_qkv,
        w_out_t,
    )


GROUPS = 8
GROUP_ROWS = 2 * CHIPS * CHUNK // GROUPS
GROUP_SLOTS = GROUP_ROWS // PARTS
EXPERT_ROWS = GROUPS * GROUP_SLOTS
DOT_ROWS = 256


def sorting(transposed):
    shape = (GROUP_ROWS, GROUP_ROWS)
    dim = 1 if transposed else 0
    quarter, row = split_index(iota(shape, dim), GROUP_SLOTS)
    row_source, row_slot = split_index(row, SLOTS)
    col_source, col = split_index(iota(shape, 1 - dim), CHUNK)
    col_quarter, col_slot = split_index(col, SLOTS)
    match = (quarter == col_quarter) & (row_source == col_source) & (row_slot == col_slot)
    return jnp.where(match, 1.0, 0.0).astype(jnp.bfloat16)


def place_pages(arrived_ref, table_ref, cache_ref):
    tok = lax.axis_index("tok")
    page, slot = split_index(table_ref[...], TOKS)
    landing = jnp.sum(jnp.where(page == tok, slot, 0).astype(jnp.float32), axis=0, keepdims=True)
    col_page, _ = split_index(iota((TOKS, TOK_ROWS), 1), PAGE_TOKENS)
    widen = jnp.where(col_page == iota((TOKS, TOK_ROWS), 0), 1.0, 0.0).astype(jnp.bfloat16)
    lands = jnp.dot(landing.astype(jnp.bfloat16), widen, preferred_element_type=jnp.float32)
    row_page, row_in = split_index(iota((TOK_ROWS, TOK_ROWS), 0), PAGE_TOKENS)
    _, col_in = split_index(iota((TOK_ROWS, TOK_ROWS), 1), PAGE_TOKENS)
    hit = (jnp.abs(lands - row_page.astype(jnp.float32)) < 0.5) & (row_in == col_in)
    pick = jnp.where(hit, 1.0, 0.0).astype(jnp.bfloat16)
    cache_ref[...] = jnp.dot(pick, arrived_ref[...], preferred_element_type=jnp.float32).astype(
        jnp.bfloat16
    )


def expert_kernel(
    recv_ref, win_ref, wdown_ref, arrived_ref, table_ref, y_ref, cache_ref, rbuf, w1, w2, xs, acts, ys, sem
):
    copies_r = [
        pltpu.make_async_copy(recv_ref.at[b], rbuf.at[b], sem.at[b]) for b in range(GROUPS)
    ]
    copy_w = pltpu.make_async_copy(win_ref, w1, sem.at[GROUPS])
    copy_d = pltpu.make_async_copy(wdown_ref, w2, sem.at[GROUPS + 1])
    for copy in copies_r + [copy_w, copy_d]:
        copy.start()
    place_pages(arrived_ref, table_ref, cache_ref)
    perm = sorting(False)
    back = sorting(True)
    for copy in copies_r:
        copy.wait()

    def sort_in(b, carry):
        mixed = jnp.dot(perm, rbuf[b], preferred_element_type=jnp.float32).astype(jnp.bfloat16)
        rows = pl.ds(pl.multiple_of(b * GROUP_SLOTS, GROUP_SLOTS), GROUP_SLOTS)
        for q in range(PARTS):
            xs[rows, q * PART_WIDTH : (q + 1) * PART_WIDTH] = mixed[
                q * GROUP_SLOTS : (q + 1) * GROUP_SLOTS
            ]
        return carry

    lax.fori_loop(0, GROUPS, sort_in, 0)
    copy_w.wait()
    contract = (((1,), (1,)), ((), ()))

    def up_block(i, carry):
        rows = pl.ds(pl.multiple_of(i * DOT_ROWS, DOT_ROWS), DOT_ROWS)
        here = xs[rows, :]
        gate = lax.dot_general(
            here, w1[:PART_WIDTH, :], contract, preferred_element_type=jnp.float32
        )
        up = lax.dot_general(
            here, w1[PART_WIDTH:, :], contract, preferred_element_type=jnp.float32
        )
        act = (up + 1.0) * gate * jax.nn.sigmoid(GLU_ALPHA * gate)
        acts[rows, :] = act.astype(jnp.bfloat16)
        return carry

    lax.fori_loop(0, EXPERT_ROWS // DOT_ROWS, up_block, 0)
    copy_d.wait()

    def down_block(i, carry):
        rows = pl.ds(pl.multiple_of(i * DOT_ROWS, DOT_ROWS), DOT_ROWS)
        down = jnp.dot(acts[rows, :], w2[...], preferred_element_type=jnp.float32)
        down = down.astype(jnp.bfloat16)
        for q in range(PARTS):
            ys[q, rows, :] = down[:, q * PART_WIDTH : (q + 1) * PART_WIDTH]
        return carry

    lax.fori_loop(0, EXPERT_ROWS // DOT_ROWS, down_block, 0)

    def sort_out(b, carry):
        rows = pl.ds(pl.multiple_of(b * GROUP_SLOTS, GROUP_SLOTS), GROUP_SLOTS)
        stacked = jnp.concatenate([ys[q, rows, :] for q in range(PARTS)], axis=0)
        y_ref[b] = jnp.dot(back, stacked, preferred_element_type=jnp.float32).astype(jnp.bfloat16)
        return carry

    lax.fori_loop(0, GROUPS, sort_out, 0)


def run_experts(received, w_in_t, w_down, arrived, table_t):
    out, cache = pl.pallas_call(
        expert_kernel,
        out_shape=(
            jax.ShapeDtypeStruct((GROUPS, GROUP_ROWS, PART_WIDTH), jnp.bfloat16),
            jax.ShapeDtypeStruct((TOK_ROWS, LANES), jnp.bfloat16),
        ),
        in_specs=[any_spec()] * 3 + [vmem_spec()] * 2,
        out_specs=(vmem_spec(), vmem_spec()),
        scratch_shapes=[
            VM((GROUPS, GROUP_ROWS, PART_WIDTH), jnp.bfloat16),
            VM((2 * PART_WIDTH, MODEL_WIDTH), jnp.bfloat16),
            VM((PART_WIDTH, MODEL_WIDTH), jnp.bfloat16),
            VM((EXPERT_ROWS, MODEL_WIDTH), jnp.bfloat16),
            VM((EXPERT_ROWS, PART_WIDTH), jnp.bfloat16),
            VM((PARTS, EXPERT_ROWS, PART_WIDTH), jnp.bfloat16),
            pltpu.SemaphoreType.DMA((GROUPS + 2,)),
        ],
        compiler_params=pltpu.CompilerParams(vmem_limit_bytes=60 << 20),
        name="run_experts",
    )(
        received.reshape(GROUPS, GROUP_ROWS, PART_WIDTH),
        w_in_t,
        w_down,
        arrived.reshape(TOK_ROWS, LANES),
        table_t,
    )
    return (out.reshape(2, CHIPS, CHUNK, PART_WIDTH), cache)


def return_kernel(y_ref, ret_ref, own, pair, sums, psend, precv, send, recv, lsem, last):
    barrier = pltpu.get_barrier_semaphore()
    sib = sibling()
    greet_all(barrier)

    def load(g):
        block = pl.ds(g * 8, 8)
        return pltpu.make_async_copy(y_ref.at[0, block], own.at[block], lsem.at[g])

    def start_load(g, carry):
        load(g).start()
        return carry

    lax.fori_loop(0, 8, start_load, 0)
    pl.semaphore_wait(barrier, CHIPS)

    def exchange(g):
        block = pl.ds(g * 8, 8)
        return remote(y_ref.at[1, block], pair.at[block], psend.at[g], precv.at[g], sib)

    def start_exchange(g, carry):
        exchange(g).start()
        return carry

    lax.fori_loop(0, 8, start_exchange, 0)

    def start_group(g):
        for i in range(g * 8, min(g * 8 + 8, CHIPS - 1)):
            remote(
                sums.at[i], ret_ref.at[i], send.at[i], recv.at[i], device(*shifted(ORDER[i], -1))
            ).start()

    for g in range(8):
        exchange(g).wait_recv()
        load(g).wait()
        block = pl.ds(g * 8, 8)
        sums[block] = (own[block].astype(jnp.float32) + pair[block].astype(jnp.float32)).astype(
            jnp.bfloat16
        )
        if g > 0:
            start_group(g - 1)
    start_group(7)
    home = pltpu.make_async_copy(sums.at[CHIPS - 1], ret_ref.at[CHIPS - 1], last)
    home.start()

    def finish_exchange(g, carry):
        exchange(g).wait_send()
        return carry

    def finish_chunk(i, carry):
        remote(sums.at[i], ret_ref.at[i], send.at[i], recv.at[i], sib).wait()
        return carry

    lax.fori_loop(0, 8, finish_exchange, 0)
    lax.fori_loop(0, CHIPS - 1, finish_chunk, 0)
    home.wait()


def give_back(y):
    return pl.pallas_call(
        return_kernel,
        out_shape=jax.ShapeDtypeStruct((CHIPS, CHUNK, PART_WIDTH), jnp.bfloat16),
        in_specs=[any_spec()],
        out_specs=any_spec(),
        scratch_shapes=[
            VM((CHIPS, CHUNK, PART_WIDTH), jnp.bfloat16),
            VM((CHIPS, CHUNK, PART_WIDTH), jnp.bfloat16),
            VM((CHIPS, CHUNK, PART_WIDTH), jnp.bfloat16),
            pltpu.SemaphoreType.DMA((8,)),
            pltpu.SemaphoreType.DMA((8,)),
            pltpu.SemaphoreType.DMA((CHIPS,)),
            pltpu.SemaphoreType.DMA((CHIPS,)),
            pltpu.SemaphoreType.DMA((8,)),
            pltpu.SemaphoreType.DMA,
        ],
        compiler_params=pltpu.CompilerParams(collective_id=3, has_side_effects=True),
        name="give_back",
    )(y)


def combine_kernel(ret_ref, resid_ref, routes_ref, gates_ref, len_ref, shift_ref, out_ref):
    x, y, z, core = place()
    live = block_live(len_ref, x * 4 + z, y * 2 + core)
    expert = iota((EXPERTS, ROWS), 0)
    gate = jnp.zeros((EXPERTS, ROWS), jnp.float32)
    for k in range(4):
        gate = gate + jnp.where(routes_ref[k : k + 1, :] == expert, gates_ref[k : k + 1, :], 0.0)
    code = expert_code(routes_ref, live)
    count = CHIPS * CHUNK
    tx, rest = split_index(shift_ref[...], 16)
    ty, tz = split_index(rest, 4)

    def wrapped(value):
        return jnp.where(value >= 4, value - 4, value)

    half = jnp.where(wrapped(ty + y) >= 2, 1, 0)
    home = (wrapped(tx + x) * 4 + wrapped(tz + z)) * 2 + half
    spread = jnp.where(iota((EXPERTS, count), 0) == home, 1.0, 0.0).astype(jnp.bfloat16)
    contract = (((0,), (0,)), ((), ()))
    code_cols = lax.dot_general(code, spread, contract, preferred_element_type=jnp.float32)
    gate_cols = lax.dot_general(
        gate.astype(jnp.bfloat16), spread, contract, preferred_element_type=jnp.float32
    )
    _, within = split_index(iota((ROWS, count), 1), CHUNK)
    quarter, slot = split_index(within, SLOTS)
    weight = jnp.where(jnp.abs(code_cols - slot.astype(jnp.float32)) < 0.5, gate_cols, 0.0)
    stacked = jnp.concatenate(
        [jnp.where(quarter == q, weight, 0.0).astype(jnp.bfloat16) for q in range(PARTS)], axis=0
    )
    total = jnp.dot(stacked, ret_ref[...], preferred_element_type=jnp.float32)
    for q in range(PARTS):
        cols = slice(q * PART_WIDTH, (q + 1) * PART_WIDTH)
        out_ref[:, cols] = (resid_ref[:, cols] + total[q * ROWS : (q + 1) * ROWS]).astype(
            jnp.bfloat16
        )


def combine(returned, resid, routes_t, gates_t, lengths):
    shifts = jnp.asarray(np.repeat(np.array(ORDER, np.int32), CHUNK)[None, :])
    return pl.pallas_call(
        combine_kernel,
        out_shape=jax.ShapeDtypeStruct((ROWS, MODEL_WIDTH), jnp.bfloat16),
        in_specs=[vmem_spec()] * 4 + [pl.BlockSpec(memory_space=pltpu.SMEM), vmem_spec()],
        out_specs=vmem_spec(),
        name="combine",
    )(returned.reshape(CHIPS * CHUNK, PART_WIDTH), resid, routes_t, gates_t, lengths, shifts)


def per_device(
    tokens,
    lengths,
    norm_gain_attn,
    query_key_value_weight,
    sinks,
    w_out_attn,
    norm_gain_moe,
    routes,
    gates,
    w_in,
    w_down,
    page_table,
):
    routes_t = jnp.transpose(routes)
    resid, received, arrived = front(
        tokens,
        norm_gain_attn,
        norm_gain_moe,
        lengths,
        routes_t,
        page_table,
        sinks,
        query_key_value_weight,
        jnp.transpose(w_out_attn),
    )
    produced, cache = run_experts(
        received, jnp.transpose(w_in[0]), w_down[0], arrived, jnp.transpose(page_table.reshape(TOKS, TOKS))
    )
    hidden_out = combine(give_back(produced), resid, routes_t, jnp.transpose(gates), lengths)
    return (hidden_out, cache.reshape(1, TOKS, PAGE_TOKENS, LANES))


def solution(mesh):
    return jax.shard_map(
        per_device,
        mesh=mesh,
        in_specs=(
            P(("tok", "head"), None),
            P(),
            P(),
            P(None, "head"),
            P("head"),
            P("head", None),
            P(),
            P(("tok", "head"), None),
            P(("tok", "head"), None),
            P(("tok", "head"), None, None),
            P(("tok", "head"), None, None),
            P(),
        ),
        out_specs=(P(("tok", "head"), None), P("head", "tok", None, None)),
        check_vma=False,
    )
```
